32 devices in a mesh: leaf: 8 (over y, x, core), row: 4 (over z).
Axes of the slice: x: 2, y: 2, z: 4, core: 2. Of those that a mesh axis runs over, the one named last changes fastest.
Arguments:
- sources_root: float32 [64, 32, 128], P('leaf'), may hold values from -6 to 6
- sources_upper: float32 [64, 32, 128], P('leaf'), may hold values from -6 to 6
- sources_middle: float32 [64, 32, 128], P('leaf'), may hold values from -6 to 6
- sources_lower: float32 [64, 32, 128], P('leaf'), may hold values from -6 to 6
- inverse_root: float32 [64, 128, 8192], P('leaf', None, 'row'), may hold values from -4 to 4, as said below
- inverse_upper: float32 [64, 128, 4096], P('leaf', None, 'row'), may hold values from -4 to 4, as said below
- inverse_middle: float32 [64, 128, 2048], P('leaf', None, 'row'), may hold values from -4 to 4, as said below
- inverse_lower: float32 [64, 128, 1024], P('leaf', None, 'row'), may hold values from -4 to 4, as said below
- update_upper: float32 [128, 128, 4096], P('leaf', None, 'row'), may hold values from -0.046875 to 0.046875
- update_middle: float32 [256, 128, 2048], P('leaf', None, 'row'), may hold values from -0.0625 to 0.0625
- update_lower: float32 [256, 128, 1024], P('leaf', None, 'row'), may hold values from -0.09375 to 0.09375
- links_upper: int32 [128], P('leaf'), may hold values from 0 to 63, as said below
- links_middle: int32 [256], P('leaf'), may hold values from 0 to 127, as said below
- links_lower: int32 [256], P('leaf'), may hold values from 0 to 191, as said below
Outputs:
- adjoint_root: float32 [64, 32, 128], P('leaf')
- adjoint_upper: float32 [64, 32, 128], P('leaf')
- adjoint_middle: float32 [64, 32, 128], P('leaf')
- adjoint_lower: float32 [64, 32, 128], P('leaf')
The draws below stay inside these ranges and needn't reach their ends.
Inputs may be any that keep to these rules, and one draw needn't show every extreme that they name: `inverse_root`: lower triangular: stored entry [g, t, p] is zero where g * 128 + t > p. `inverse_upper`: lower triangular: stored entry [g, t, p] is zero where (g % 32) * 128 + t > p. `inverse_middle`: lower triangular: stored entry [g, t, p] is zero where (g % 16) * 128 + t > p. `inverse_lower`: lower triangular: stored entry [g, t, p] is zero where (g % 8) * 128 + t > p. `links_upper`: the entries of one front are distinct and all belong to the root front. `links_middle`: the entries of one front are distinct and belong to the front's own ancestors (the root and its parent of level 1). `links_lower`: the entries of one front are distinct and belong to the front's own ancestors on levels 0 to 2.
All inputs are finite; a program needn't handle non-finite values.
Results may differ from the reference program's by a relative error of at most 0.00014.
Values sent between devices are 32-bit elements; how exact they have to be, the bound alone decides.
A program may use at most 128 MiB of HBM per device.

```python
import math
import jax
import jax.numpy as jnp
from jax import lax

PIV_ROOT = 8192
BLOCK_ROWS = 128
RESIDUALS = 32
PIV_UPPER = 4096
PIV_MIDDLE = 2048
PIV_LOWER = 1024
UPD_UPPER = 8192
UPD_MIDDLE = 8192
UPD_LOWER = 4096


def make_inverse(base_key, fronts, pivots):
    shape = (fronts, pivots // BLOCK_ROWS, BLOCK_ROWS, pivots)
    column = lax.broadcasted_iota(jnp.int32, shape, 1) * BLOCK_ROWS + lax.broadcasted_iota(jnp.int32, shape, 2)
    row_index = lax.broadcasted_iota(jnp.int32, shape, 3)
    first, second = jax.random.split(base_key, 2)
    beside = jax.random.normal(first, shape, jnp.float32) * (0.5 / math.sqrt(pivots))
    diagonal = jax.random.uniform(second, shape, jnp.float32, 0.8, 1.6)
    values = jnp.where(column == row_index, diagonal, jnp.where(column < row_index, beside, 0.0))
    return values.astype(jnp.float32).reshape(fronts * (pivots // BLOCK_ROWS), BLOCK_ROWS, pivots)


def make_links(base_key, level_in_tree, fronts, amount):
    blocks = PIV_ROOT // BLOCK_ROWS

    def single(front_key, front):
        pieces = []
        for upper_level in range(level_in_tree):
            across = (PIV_ROOT >> upper_level) // BLOCK_ROWS
            owner = jnp.right_shift(front, level_in_tree - upper_level)
            pieces.append(upper_level * blocks + owner * across + jnp.arange(across, dtype=jnp.int32))
        candidates = jnp.concatenate(pieces)
        shuffled = jax.random.permutation(front_key, candidates.shape[0])
        return candidates[shuffled[:amount]].astype(jnp.int32)
    front_keys = jax.random.split(base_key, fronts)
    return jax.vmap(single)(front_keys, jnp.arange(fronts, dtype=jnp.int32)).reshape(-1)


def draw_inverse_root(key, part):
    return make_inverse(jax.random.fold_in(key, 101), 1, PIV_ROOT)


def draw_inverse_upper(key, part):
    return make_inverse(jax.random.fold_in(key, 102), 2, PIV_UPPER)


def draw_inverse_middle(key, part):
    return make_inverse(jax.random.fold_in(key, 103), 4, PIV_MIDDLE)


def draw_inverse_lower(key, part):
    return make_inverse(jax.random.fold_in(key, 104), 8, PIV_LOWER)


def draw_links_upper(key, part):
    return make_links(jax.random.fold_in(key, 201), 1, 2, UPD_UPPER // BLOCK_ROWS)


def draw_links_middle(key, part):
    return make_links(jax.random.fold_in(key, 202), 2, 4, UPD_MIDDLE // BLOCK_ROWS)


def draw_links_lower(key, part):
    return make_links(jax.random.fold_in(key, 203), 3, 8, UPD_LOWER // BLOCK_ROWS)


def shard_levels(key, extent, cuts, smallest, high):
    level = 1.0
    for axis_at, parts in cuts:
        heights = jax.random.uniform(jax.random.fold_in(jax.random.fold_in(key, 6), axis_at), (parts,), jnp.float32, smallest / len(cuts), high / len(cuts))
        level = level * jnp.repeat(jnp.exp(heights), extent[axis_at] // parts).reshape((-1,) + (1,) * (len(extent) - 1 - axis_at))
    return level


def noise(own_key, dims, width, reach, cuts=(), held_as=jnp.bfloat16):
    loudness = shard_levels(own_key, dims, cuts, -0.22, 0.18) if cuts else 1.0
    values = jax.random.normal(own_key, dims, jnp.float32) * width * loudness
    return jnp.minimum(jnp.maximum(values, -reach), reach).astype(held_as)


def setup_inputs(seed: int = 0) -> dict:
    keys = jax.random.split(jax.random.key(seed), 15)
    return {
        "sources_root": noise(keys[0], (PIV_ROOT // BLOCK_ROWS, RESIDUALS, BLOCK_ROWS), 1.0, 6.0, ((0, 8),), jnp.float32),
        "sources_upper": noise(keys[1], (PIV_ROOT // BLOCK_ROWS, RESIDUALS, BLOCK_ROWS), 1.0, 6.0, ((0, 8),), jnp.float32),
        "sources_middle": noise(keys[2], (PIV_ROOT // BLOCK_ROWS, RESIDUALS, BLOCK_ROWS), 1.0, 6.0, ((0, 8),), jnp.float32),
        "sources_lower": noise(keys[3], (PIV_ROOT // BLOCK_ROWS, RESIDUALS, BLOCK_ROWS), 1.0, 6.0, ((0, 8),), jnp.float32),
        "inverse_root": draw_inverse_root(jax.random.fold_in(keys[14], 71), 0),
        "inverse_upper": draw_inverse_upper(jax.random.fold_in(keys[14], 71), 0),
        "inverse_middle": draw_inverse_middle(jax.random.fold_in(keys[14], 71), 0),
        "inverse_lower": draw_inverse_lower(jax.random.fold_in(keys[14], 71), 0),
        "update_upper": noise(keys[8], (2 * UPD_UPPER // BLOCK_ROWS, BLOCK_ROWS, PIV_UPPER), (4 * PIV_UPPER) ** -0.5, 0.046875, ((0, 8), (2, 4)), jnp.float32),
        "update_middle": noise(keys[9], (4 * UPD_MIDDLE // BLOCK_ROWS, BLOCK_ROWS, PIV_MIDDLE), (4 * PIV_MIDDLE) ** -0.5, 0.0625, ((0, 8), (2, 4)), jnp.float32),
        "update_lower": noise(keys[10], (8 * UPD_LOWER // BLOCK_ROWS, BLOCK_ROWS, PIV_LOWER), (4 * PIV_LOWER) ** -0.5, 0.09375, ((0, 8), (2, 4)), jnp.float32),
        "links_upper": draw_links_upper(jax.random.fold_in(keys[14], 71), 0),
        "links_middle": draw_links_middle(jax.random.fold_in(keys[14], 71), 0),
        "links_lower": draw_links_lower(jax.random.fold_in(keys[14], 71), 0),
    }


def reference(sources_root, sources_upper, sources_middle, sources_lower, inverse_root, inverse_upper, inverse_middle, inverse_lower, update_upper, update_middle, update_lower, links_upper, links_middle, links_lower):
    highest = lax.Precision.HIGHEST
    blocks = PIV_ROOT // BLOCK_ROWS
    pivots = [PIV_ROOT, PIV_UPPER, PIV_MIDDLE, PIV_LOWER]
    uppers = [0, UPD_UPPER, UPD_MIDDLE, UPD_LOWER]
    raw_sources = [sources_root, sources_upper, sources_middle, sources_lower]
    raw_inverse = [inverse_root, inverse_upper, inverse_middle, inverse_lower]
    raw_update = [None, update_upper, update_middle, update_lower]
    raw_links = [None, links_upper, links_middle, links_lower]
    sources = [raw_sources[level].reshape(1 << level, pivots[level] // BLOCK_ROWS, RESIDUALS, BLOCK_ROWS) for level in range(4)]
    inverse_factor = [raw_inverse[level].reshape(1 << level, pivots[level] // BLOCK_ROWS, BLOCK_ROWS, pivots[level]) for level in range(4)]
    update = [None] + [raw_update[level].reshape(1 << level, uppers[level] // BLOCK_ROWS, BLOCK_ROWS, pivots[level]) for level in range(1, 4)]
    links = [None] + [raw_links[level].reshape(1 << level, uppers[level] // BLOCK_ROWS) for level in range(1, 4)]
    pending = [jnp.zeros((blocks, RESIDUALS, BLOCK_ROWS), jnp.float32) for level_in_tree in range(4)]
    forward = [None, None, None, None]
    for level_in_tree in (3, 2, 1, 0):
        source_vector = sources[level_in_tree] - pending[level_in_tree].reshape(sources[level_in_tree].shape)
        solved = jnp.einsum("fbtp,fbrt->frp", inverse_factor[level_in_tree], source_vector, precision=highest)
        forward[level_in_tree] = solved
        if level_in_tree > 0:
            matrix_product = jnp.einsum("fktp,frp->fkrt", update[level_in_tree], solved, precision=highest)
            stacked_terms = matrix_product.reshape(-1, RESIDUALS, BLOCK_ROWS)
            target = links[level_in_tree].reshape(-1).astype(jnp.int32)
            spread = jnp.zeros((level_in_tree * blocks, RESIDUALS, BLOCK_ROWS), jnp.float32).at[target].add(stacked_terms)
            for upper_level in range(level_in_tree):
                pending[upper_level] = pending[upper_level] + spread[upper_level * blocks:(upper_level + 1) * blocks]
    solutions = [None, None, None, None]
    for level_in_tree in range(4):
        fixed_update = forward[level_in_tree]
        if level_in_tree > 0:
            stacked = jnp.concatenate([solutions[upper_level].reshape(blocks, RESIDUALS, BLOCK_ROWS) for upper_level in range(level_in_tree)], axis=0)
            picked = stacked[links[level_in_tree].astype(jnp.int32)]
            backward = jnp.einsum("fktp,fkrt->frp", update[level_in_tree], picked, precision=highest)
            fixed_update = fixed_update - backward
        solutions[level_in_tree] = jnp.einsum("fbtp,frp->fbrt", inverse_factor[level_in_tree], fixed_update, precision=highest)
    outputs = [solutions[level].reshape(blocks, RESIDUALS, BLOCK_ROWS) for level in range(4)]
    return (outputs[0], outputs[1], outputs[2], outputs[3])
```

```python
import functools

import jax
import jax.numpy as jnp
from jax import lax
from jax.experimental import pallas as pl
from jax.experimental.pallas import tpu as pltpu
from jax.sharding import PartitionSpec as P

LANES = 128
SUB = 8
MESH = pl.DeviceIdType.MESH
LEVELS = 4


def split(x):
    hi = x.astype(jnp.bfloat16)
    lo = (x - hi.astype(jnp.float32)).astype(jnp.bfloat16)
    return hi, lo


def kernel(cfg, *refs):
    L, R = cfg["L"], cfg["R"]
    nT = cfg["nT"]
    rhs = cfg["rhs"]
    TB = rhs // SUB
    cols = cfg["cols"]
    nb = cfg["nb"]
    base = cfg["base"]
    it = iter(refs)
    index_ref = next(it)
    src_hbm = [next(it) for _ in range(LEVELS)]
    inv_hbm = [next(it) for _ in range(LEVELS)]
    upd_hbm = [None] + [next(it) for _ in range(LEVELS - 1)]
    out_hbm = [next(it) for _ in range(LEVELS)]
    src = [next(it) for _ in range(LEVELS)]
    inv = [next(it) for _ in range(LEVELS)]
    upd = [None] + [next(it) for _ in range(LEVELS - 1)]
    c_buf = next(it)
    pend = next(it)
    stack = next(it)
    w_split = next(it)
    y_split = next(it)
    y_part = next(it)
    y_full = [next(it) for _ in range(LEVELS)]
    z_part = next(it)
    s_full = [None] + [next(it) for _ in range(LEVELS - 1)]
    load_sem = next(it)
    out_sem = next(it)
    phases = {}
    for name, _, _ in cfg["phases"]:
        phases[name] = next(it)
    send_sem = next(it)
    recv_sem = next(it)
    phase_at = {name: i for i, (name, _, _) in enumerate(cfg["phases"])}

    leaf = lax.axis_index("leaf")
    row = lax.axis_index("row")

    loads = {}
    at = 0
    for d in reversed(range(LEVELS)):
        for tag, a, b in (("s", src_hbm, src), ("i", inv_hbm, inv), ("u", upd_hbm, upd)):
            if a[d] is None:
                continue
            copy = pltpu.make_async_copy(a[d], b[d], load_sem.at[at])
            copy.start()
            loads[tag, d] = copy
            at += 1

    barrier = pltpu.get_barrier_semaphore()
    for k in range(1, L):
        pl.semaphore_signal(barrier, inc=1, device_id=((leaf + k) % L, row), device_id_type=MESH)
    for k in range(1, R):
        pl.semaphore_signal(barrier, inc=1, device_id=(leaf, (row + k) % R), device_id_type=MESH)
    pl.semaphore_wait(barrier, L + R - 2)

    def leaf_group(d):
        G = L >> d
        first = (leaf // G) * G
        me = leaf % G
        return G, me, lambda other: (first + other, row)

    row_group = (R, row, lambda other: (leaf, other))

    def tiles(ref, start, n):
        return ref.at[pl.ds(start, n)]

    def wait_all(name, ref, n):
        i = phase_at[name]
        whole = ref.at[pl.ds(0, n)]
        pltpu.make_async_copy(whole, whole, recv_sem.at[i]).wait()
        pltpu.make_async_copy(whole, whole, send_sem.at[i]).wait()

    def reduce_scatter(name, group, source, at0, n, target, to):
        G, me, who = group
        recv = phases[name]
        i = phase_at[name]
        for k in range(1, G):
            other = (me + k) % G
            pltpu.make_async_remote_copy(
                src_ref=tiles(source, at0 + other * n, n),
                dst_ref=tiles(recv, (k - 1) * n, n),
                send_sem=send_sem.at[i],
                recv_sem=recv_sem.at[i],
                device_id=who(other),
                device_id_type=MESH,
            ).start()
        if G > 1:
            wait_all(name, recv, (G - 1) * n)
        total = source[pl.ds(at0 + me * n, n)]
        for k in range(1, G):
            total = total + recv[pl.ds((k - 1) * n, n)]
        target[pl.ds(to, n)] = total

    def all_gather(name, group, full, n):
        G, me, who = group
        i = phase_at[name]
        for k in range(1, G):
            other = (me + k) % G
            pltpu.make_async_remote_copy(
                src_ref=tiles(full, me * n, n),
                dst_ref=tiles(full, me * n, n),
                send_sem=send_sem.at[i],
                recv_sem=recv_sem.at[i],
                device_id=who(other),
                device_id_type=MESH,
            ).start()
        if G > 1:
            wait_all(name, full, (G - 1) * n)

    def put_w(pair, half, block):
        hi, lo = split(block)
        w_split[pair, 0:rhs, half * LANES:(half + 1) * LANES] = hi
        w_split[pair, rhs:2 * rhs, half * LANES:(half + 1) * LANES] = lo

    def fill_y(values, d):
        for cb in range(cols[d] // LANES):
            hi, lo = split(values(cb))
            y_split[0:rhs, cb * LANES:(cb + 1) * LANES] = hi
            y_split[rhs:2 * rhs, cb * LANES:(cb + 1) * LANES] = lo

    def block_of(ref, b):
        return ref[pl.ds(b * TB, TB)].reshape(rhs, LANES)

    def over_rows(mat, rows, width, target):
        step = min(512, width)
        for nt in range(width // step):
            def body(k, acc):
                m = mat[pl.ds(k * 256, 256), nt * step:(nt + 1) * step]
                hi, lo = split(m)
                w = w_split[k]
                p = jnp.dot(w, hi, preferred_element_type=jnp.float32)
                q = jnp.dot(w[:rhs], lo, preferred_element_type=jnp.float32)
                return acc + (p[:rhs] + (p[rhs:] + q))
            acc = lax.fori_loop(0, rows // 256, body, jnp.zeros((rhs, step), jnp.float32), unroll=2 if rows >= 512 else 1)
            for c in range(step // LANES):
                target[pl.ds((nt * (step // LANES) + c) * TB, TB)] = acc[:, c * LANES:(c + 1) * LANES].reshape(TB, SUB, LANES)

    def over_cols(mat, rows, width, target):
        step = min(512, width)
        dims = (((1,), (1,)), ((), ()))

        def body(rt, carry):
            acc = jnp.zeros((rhs, 256), jnp.float32)
            for pc in range(width // step):
                m = mat[pl.ds(rt * 256, 256), pc * step:(pc + 1) * step]
                hi, lo = split(m)
                y = y_split[:, pc * step:(pc + 1) * step]
                p = lax.dot_general(y, hi, dims, preferred_element_type=jnp.float32)
                q = lax.dot_general(y[:rhs], lo, dims, preferred_element_type=jnp.float32)
                acc = acc + (p[:rhs] + (p[rhs:] + q))
            target[pl.ds(rt * 2 * TB, TB)] = acc[:, :LANES].reshape(TB, SUB, LANES)
            target[pl.ds(rt * 2 * TB + TB, TB)] = acc[:, LANES:].reshape(TB, SUB, LANES)
            return carry

        lax.fori_loop(0, rows // 256, body, 0, unroll=2 if rows >= 512 else 1)

    own_blocks = nT // TB
    zn = nT // R
    for d in reversed(range(LEVELS)):
        group = leaf_group(d)
        G, me, _ = group
        loads["s", d].wait()
        if d < LEVELS - 1:
            reduce_scatter(f"pend{d}", group, pend, base[d], nT, z_part, 0)
            full = phases[f"wg{d}"]
            reduce_scatter(f"wr{d}", row_group, z_part, 0, zn, full, row * zn)
            all_gather(f"wg{d}", row_group, full, zn)
        for b in range(own_blocks):
            w = block_of(src[d], b)
            if d < LEVELS - 1:
                w = w - block_of(full, b)
            put_w(b // 2, b % 2, w)
        loads["i", d].wait()
        yn = cols[d] // LANES * TB // G
        if G > 1:
            over_rows(inv[d], nT // TB * LANES, cols[d], y_part)
            reduce_scatter(f"yr{d}", group, y_part, 0, yn, y_full[d], me * yn)
            all_gather(f"yg{d}", group, y_full[d], yn)
        else:
            over_rows(inv[d], nT // TB * LANES, cols[d], y_full[d])
        fill_y(lambda cb: block_of(y_full[d], cb), d)
        if d > 0:
            loads["u", d].wait()
            over_cols(upd[d], nb[d] * LANES, cols[d], c_buf)
            c_buf[pl.ds(nb[d] * TB, TB)] = jnp.zeros((TB, SUB, LANES), jnp.float32)
            first = cfg["inv_at"][d]

            def scatter(b, carry):
                j = index_ref[first + b]
                term = c_buf[pl.ds(j * TB, TB)]
                where = pl.ds(b * TB, TB)
                if d < LEVELS - 1:
                    term = pend[where] + term
                pend[where] = term
                return carry

            lax.fori_loop(0, base[d] // TB, scatter, 0, unroll=2)

    finals = []
    for d in range(LEVELS):
        group = leaf_group(d)
        G, me, _ = group
        if d > 0:
            first = cfg["idx_at"][d]

            def gather(pair, carry):
                for half in range(2):
                    b = index_ref[first + pair * 2 + half]
                    put_w(pair, half, stack[pl.ds(b * TB, TB)].reshape(rhs, LANES))
                return carry

            lax.fori_loop(0, nb[d] // 2, gather, 0, unroll=2)
            yn = cols[d] // LANES * TB // G
            if G > 1:
                over_rows(upd[d], nb[d] * LANES, cols[d], y_part)
                reduce_scatter(f"sr{d}", group, y_part, 0, yn, s_full[d], me * yn)
                all_gather(f"sg{d}", group, s_full[d], yn)
            else:
                over_rows(upd[d], nb[d] * LANES, cols[d], s_full[d])
            fill_y(lambda cb: block_of(y_full[d], cb) - block_of(s_full[d], cb), d)
        over_cols(inv[d], nT // TB * LANES, cols[d], z_part)
        full = phases[f"ag{d}"]
        reduce_scatter(f"ar{d}", row_group, z_part, 0, zn, full, row * zn)
        all_gather(f"ag{d}", row_group, full, zn)
        final = pltpu.make_async_copy(full, out_hbm[d], out_sem.at[d])
        final.start()
        finals.append(final)
        if d < LEVELS - 1:
            front = phases[f"fg{d}"]
            front[pl.ds(me * nT, nT)] = full[...]
            all_gather(f"fg{d}", group, front, nT)
            stack[pl.ds(base[d], G * nT)] = front[...]
    for final in finals:
        final.wait()


def make_body(L, R):
    def body(*args):
        sources, inverse, update, links = args[0:4], args[4:8], (None,) + args[8:11], (None,) + args[11:14]
        own, rhs, lanes = sources[0].shape
        TB = rhs // SUB
        nT = own * TB
        blocks = own * L
        counts = [blocks >> d for d in range(LEVELS)]
        bases = [sum(counts[:d]) for d in range(LEVELS)]
        cols = [a.shape[2] for a in inverse]
        nb = [0] + [a.shape[0] for a in update[1:]]

        pieces = []
        idx_at, inv_at = [0] * LEVELS, [0] * LEVELS
        at = 0
        for d in range(1, LEVELS):
            link = links[d].astype(jnp.int32)
            level = link // blocks
            idx = jnp.zeros_like(link)
            for u in range(d):
                idx = jnp.where(level == u, bases[u] + link % counts[u], idx)
            idx_at[d] = at
            at += nb[d]
            number = jnp.arange(nb[d], dtype=jnp.int32)
            hits = idx[:, None] == jnp.arange(bases[d], dtype=jnp.int32)[None, :]
            inverse_map = nb[d] + jnp.sum(jnp.where(hits, (number - nb[d])[:, None], 0), axis=0)
            inv_at[d] = at
            at += bases[d]
            pieces += [idx, inverse_map.astype(jnp.int32)]
        index = jnp.concatenate(pieces)

        tile = lambda n: (n, SUB, LANES)
        phases = []
        for d in range(LEVELS):
            G = L >> d
            yt = cols[d] // LANES * TB
            if d < LEVELS - 1:
                phases.append((f"pend{d}", (G - 1) * nT, True))
                phases.append((f"wr{d}", (R - 1) * (nT // R), True))
                phases.append((f"wg{d}", nT, True))
                phases.append((f"fg{d}", G * nT, True))
            if G > 1:
                phases.append((f"yr{d}", (G - 1) * (yt // G), True))
                phases.append((f"yg{d}", 1, False))
                if d > 0:
                    phases.append((f"sr{d}", (G - 1) * (yt // G), True))
                    phases.append((f"sg{d}", 1, False))
            phases.append((f"ar{d}", (R - 1) * (nT // R), True))
            phases.append((f"ag{d}", nT, True))
        cfg = dict(
            L=L, R=R, nT=nT, rhs=rhs, cols=cols, nb=nb, base=[b * TB for b in bases],
            idx_at=idx_at, inv_at=inv_at, phases=phases,
        )
        f32 = jnp.float32
        max_cols = max(cols)
        max_rows = max(max(nb), own)
        scratch = []
        scratch += [pltpu.VMEM(tile(nT), f32) for _ in range(LEVELS)]
        scratch += [pltpu.VMEM((a.shape[0] * a.shape[1], a.shape[2]), f32) for a in inverse]
        scratch += [pltpu.VMEM((a.shape[0] * a.shape[1], a.shape[2]), f32) for a in update[1:]]
        scratch.append(pltpu.VMEM(tile((max(nb) + 1) * TB), f32))
        scratch.append(pltpu.VMEM(tile(bases[-1] * TB), f32))
        scratch.append(pltpu.VMEM(tile(bases[-1] * TB), f32))
        scratch.append(pltpu.VMEM((max_rows // 2, 2 * rhs, 2 * LANES), jnp.bfloat16))
        scratch.append(pltpu.VMEM((2 * rhs, max_cols), jnp.bfloat16))
        scratch.append(pltpu.VMEM(tile(max_cols // LANES * TB), f32))
        scratch += [pltpu.VMEM(tile(cols[d] // LANES * TB), f32) for d in range(LEVELS)]
        scratch.append(pltpu.VMEM(tile(nT), f32))
        scratch += [pltpu.VMEM(tile(cols[d] // LANES * TB), f32) for d in range(1, LEVELS)]
        scratch.append(pltpu.SemaphoreType.DMA((3 * LEVELS,)))
        scratch.append(pltpu.SemaphoreType.DMA((LEVELS,)))
        scratch += [pltpu.VMEM(tile(n), f32) for _, n, _ in phases]
        scratch.append(pltpu.SemaphoreType.DMA((len(phases),)))
        scratch.append(pltpu.SemaphoreType.DMA((len(phases),)))

        operands = [index]
        operands += [a.reshape(tile(nT)) for a in sources]
        operands += [a.reshape(-1, a.shape[2]) for a in inverse]
        operands += [a.reshape(-1, a.shape[2]) for a in update[1:]]
        anywhere = pl.BlockSpec(memory_space=pl.ANY)
        outs = pl.pallas_call(
            functools.partial(kernel, cfg),
            name="solve",
            out_shape=[jax.ShapeDtypeStruct(tile(nT), f32)] * LEVELS,
            in_specs=[pl.BlockSpec(memory_space=pltpu.SMEM)] + [anywhere] * (len(operands) - 1),
            out_specs=[anywhere] * LEVELS,
            scratch_shapes=scratch,
            compiler_params=pltpu.CompilerParams(
                collective_id=0, has_side_effects=True, vmem_limit_bytes=67043328 - (1 << 20)
            ),
        )(*operands)
        return tuple(o.reshape(own, rhs, lanes) for o in outs)

    return body


def solution(mesh):
    rows = P("leaf", None, None)
    factor = P("leaf", None, "row")
    return jax.shard_map(
        make_body(mesh.shape["leaf"], mesh.shape["row"]),
        mesh=mesh,
        in_specs=(rows,) * 4 + (factor,) * 7 + (P("leaf"),) * 3,
        out_specs=(rows,) * 4,
        check_vma=False,
    )
```

```python
import functools

import jax
import jax.numpy as jnp
from jax import lax
from jax.experimental import pallas as pl
from jax.experimental.pallas import tpu as pltpu
from jax.sharding import PartitionSpec as P

LANES = 128
SUB = 8
MESH = pl.DeviceIdType.MESH
LEVELS = 4


def split(x):
    hi = x.astype(jnp.bfloat16)
    lo = (x - hi.astype(jnp.float32)).astype(jnp.bfloat16)
    return hi, lo


def kernel(cfg, *refs):
    L, R = cfg["L"], cfg["R"]
    nT = cfg["nT"]
    rhs = cfg["rhs"]
    TB = rhs // SUB
    cols = cfg["cols"]
    nb = cfg["nb"]
    base = cfg["base"]
    it = iter(refs)
    index_ref = next(it)
    src_hbm = [next(it) for _ in range(LEVELS)]
    inv_hbm = [next(it) for _ in range(LEVELS)]
    upd_hbm = [None] + [next(it) for _ in range(LEVELS - 1)]
    out_hbm = [next(it) for _ in range(LEVELS)]
    src = [next(it) for _ in range(LEVELS)]
    inv = [next(it) for _ in range(LEVELS)]
    upd = [None] + [next(it) for _ in range(LEVELS - 1)]
    c_buf = next(it)
    pend = next(it)
    stack = next(it)
    w_split = next(it)
    y_split = next(it)
    y_part = next(it)
    y_full = [next(it) for _ in range(LEVELS)]
    z_part = next(it)
    s_full = [None] + [next(it) for _ in range(LEVELS - 1)]
    load_sem = next(it)
    out_sem = next(it)
    phases = {}
    for name, _ in cfg["phases"]:
        phases[name] = next(it)
    sems = next(it)

    leaf = lax.axis_index("leaf")
    row = lax.axis_index("row")

    loads = {}
    at = 0
    for d in reversed(range(LEVELS)):
        for tag, a, b in (("s", src_hbm, src), ("i", inv_hbm, inv), ("u", upd_hbm, upd)):
            if a[d] is None:
                continue
            copy = pltpu.make_async_copy(a[d], b[d], load_sem.at[at])
            copy.start()
            loads[tag, d] = copy
            at += 1

    barrier = pltpu.get_barrier_semaphore()
    for k in range(1, L):
        pl.semaphore_signal(barrier, inc=1, device_id=((leaf + k) % L, row), device_id_type=MESH)
    for k in range(1, R):
        pl.semaphore_signal(barrier, inc=1, device_id=(leaf, (row + k) % R), device_id_type=MESH)
    pl.semaphore_wait(barrier, L + R - 2)

    def leaf_group(d):
        G = L >> d
        first = (leaf // G) * G
        me = leaf % G
        return G, me, lambda other: (first + other, row)

    def tiles(ref, start, n):
        return ref.at[pl.ds(start, n)]

    counter = [0]

    def new_sem():
        counter[0] += 1
        return sems.at[counter[0] - 1]

    def wait_tiles(sem, ref, n):
        whole = ref.at[pl.ds(0, n)]
        pltpu.make_async_copy(whole, whole, sem).wait()

    def push(source, target, out_s, in_s, device):
        pltpu.make_async_remote_copy(
            src_ref=source,
            dst_ref=target,
            send_sem=out_s,
            recv_sem=in_s,
            device_id=device,
            device_id_type=MESH,
        ).start()

    def group_sum(name, group, source, total_tiles, target):
        G, me, who = group
        recv = phases[name]
        if G == 2:
            out_s, in_s = new_sem(), new_sem()
            push(tiles(source, 0, total_tiles), tiles(recv, 0, total_tiles), out_s, in_s, who(1 - me))
            wait_tiles(in_s, recv, total_tiles)
            target[...] = source[pl.ds(0, total_tiles)] + recv[...]
            wait_tiles(out_s, recv, total_tiles)
            return
        n = total_tiles // G
        out_s, in_s = new_sem(), new_sem()
        for k in range(1, G):
            other = (me + k) % G
            push(tiles(source, other * n, n), tiles(recv, (k - 1) * n, n), out_s, in_s, who(other))
        wait_tiles(in_s, recv, (G - 1) * n)
        total = source[pl.ds(me * n, n)]
        for k in range(1, G):
            total = total + recv[pl.ds((k - 1) * n, n)]
        target[pl.ds(me * n, n)] = total
        wait_tiles(out_s, recv, (G - 1) * n)
        out_s, in_s = new_sem(), new_sem()
        for k in range(1, G):
            mine = tiles(target, me * n, n)
            push(mine, mine, out_s, in_s, who((me + k) % G))
        wait_tiles(in_s, target, (G - 1) * n)
        wait_tiles(out_s, target, (G - 1) * n)

    C, cn = cfg["C"], nT // cfg["C"]
    half_row = R // 2
    right = row // half_row
    inward = row + 1 - 2 * right
    outward = row - 1 + 2 * right
    depth = (half_row - 1 - row) * (1 - right) + (row - half_row) * right

    def row_sum(name, prepare, done):
        came, across, full = phases[name + "i"], phases[name + "x"], phases[name + "f"]
        out_in, out_back = new_sem(), new_sem()
        in_s = [new_sem() for _ in range(C)]
        x_s = [new_sem() for _ in range(C)]
        f_s = [new_sem() for _ in range(C)]
        for c in range(C):
            part = tiles(z_part, c * cn, cn)
            prepare(c)
            if half_row > 1:
                @pl.when(depth < half_row - 1)
                def _():
                    wait_tiles(in_s[c], came, cn)
                    z_part[pl.ds(c * cn, cn)] = z_part[pl.ds(c * cn, cn)] + came[pl.ds(c * cn, cn)]

                @pl.when(depth > 0)
                def _():
                    push(part, tiles(came, c * cn, cn), out_in, in_s[c], (leaf, inward))

            @pl.when(depth == 0)
            def _():
                push(part, tiles(across, c * cn, cn), out_in, x_s[c], (leaf, inward))
        for c in range(C):
            here = tiles(full, c * cn, cn)

            @pl.when(depth == 0)
            def _():
                wait_tiles(x_s[c], across, cn)
                full[pl.ds(c * cn, cn)] = z_part[pl.ds(c * cn, cn)] + across[pl.ds(c * cn, cn)]

            if half_row > 1:
                @pl.when(depth > 0)
                def _():
                    wait_tiles(f_s[c], full, cn)

                @pl.when(depth < half_row - 1)
                def _():
                    push(here, here, out_back, f_s[c], (leaf, outward))
            done(c, full)

        def finish():
            wait_tiles(out_in, full, nT)
            if half_row > 1:
                @pl.when(depth < half_row - 1)
                def _():
                    wait_tiles(out_back, full, nT)

        return full, finish

    def pend_scatter(d, group):
        G, me, who = group
        H, chip, core = G // 2, me // 2, me % 2
        from_core, from_chip = phases[f"pc{d}"], phases[f"ph{d}"]
        out_core, out_chip = new_sem(), new_sem()
        core_s = [new_sem() for _ in range(H)]
        chip_s = [new_sem() for _ in range(C)]
        for k in list(range(1, H)) + [0]:
            ch = (chip + k) % H
            push(tiles(pend, base[d] + (2 * ch + 1 - core) * nT, nT), tiles(from_core, k * nT, nT), out_core, core_s[k], who(2 * chip + 1 - core))
        for c in range(C):
            for k in range(1, H):
                ch = (chip + k) % H
                if c == 0:
                    wait_tiles(core_s[k], from_core, nT)
                where = pl.ds(base[d] + (2 * ch + core) * nT + c * cn, cn)
                pend[where] = pend[where] + from_core[pl.ds(k * nT + c * cn, cn)]
                push(pend.at[where], tiles(from_chip, (k - 1) * nT + c * cn, cn), out_chip, chip_s[c], who(2 * ch + core))

        def prepare(c):
            if c == 0:
                wait_tiles(core_s[0], from_core, nT)
            total = pend[pl.ds(base[d] + me * nT + c * cn, cn)] + from_core[pl.ds(c * cn, cn)]
            if H > 1:
                wait_tiles(chip_s[c], from_chip, (H - 1) * cn)
            for k in range(1, H):
                total = total + from_chip[pl.ds((k - 1) * nT + c * cn, cn)]
            z_part[pl.ds(c * cn, cn)] = total

        def finish():
            wait_tiles(out_core, pend, H * nT)
            if H > 1:
                wait_tiles(out_chip, pend, (H - 1) * nT)

        return prepare, finish

    def front_gather(d, group):
        G, me, who = group
        H, chip, core = G // 2, me // 2, me % 2
        front = phases[f"fg{d}"]
        out_s, core_s = new_sem(), new_sem()
        chip_s = [new_sem() for _ in range(C)]
        partner = who(2 * chip + 1 - core)

        def done(c, full):
            mine = tiles(full, c * cn, cn)
            target = tiles(front, me * nT + c * cn, cn)
            for k in range(1, H):
                push(mine, target, out_s, chip_s[c], who(2 * ((chip + k) % H) + core))
            push(mine, target, out_s, core_s, partner)
            front[pl.ds(me * nT + c * cn, cn)] = full[pl.ds(c * cn, cn)]

        def finish():
            for c in range(C):
                if H > 1:
                    wait_tiles(chip_s[c], front, (H - 1) * cn)
                for k in range(1, H):
                    other = 2 * ((chip + k) % H) + core
                    piece = tiles(front, other * nT + c * cn, cn)
                    push(piece, piece, out_s, core_s, partner)
            wait_tiles(core_s, front, H * nT)
            wait_tiles(out_s, front, (2 * H - 1) * nT)
            stack[pl.ds(base[d], G * nT)] = front[...]

        return done, finish

    def put_w(pair, half, block):
        hi, lo = split(block)
        w_split[pair, 0:rhs, half * LANES:(half + 1) * LANES] = hi
        w_split[pair, rhs:2 * rhs, half * LANES:(half + 1) * LANES] = lo

    def fill_y(values, d):
        for cb in range(cols[d] // LANES):
            hi, lo = split(values(cb))
            y_split[0:rhs, cb * LANES:(cb + 1) * LANES] = hi
            y_split[rhs:2 * rhs, cb * LANES:(cb + 1) * LANES] = lo

    def block_of(ref, b):
        return ref[pl.ds(b * TB, TB)].reshape(rhs, LANES)

    def over_rows(mat, rows, width, target):
        step = min(512, width)
        for nt in range(width // step):
            def body(k, acc):
                m = mat[pl.ds(k * 256, 256), nt * step:(nt + 1) * step]
                hi, lo = split(m)
                w = w_split[k]
                p = jnp.dot(w, hi, preferred_element_type=jnp.float32)
                q = jnp.dot(w[:rhs], lo, preferred_element_type=jnp.float32)
                return acc + (p[:rhs] + (p[rhs:] + q))
            acc = lax.fori_loop(0, rows // 256, body, jnp.zeros((rhs, step), jnp.float32), unroll=2 if rows >= 512 else 1)
            for c in range(step // LANES):
                target[pl.ds((nt * (step // LANES) + c) * TB, TB)] = acc[:, c * LANES:(c + 1) * LANES].reshape(TB, SUB, LANES)

    def over_cols(mat, rows, width, target, chunk=None):
        step = min(512, width)
        dims = (((1,), (1,)), ((), ()))

        def body(rt, carry):
            acc = jnp.zeros((rhs, 256), jnp.float32)
            for pc in range(width // step):
                m = mat[pl.ds(rt * 256, 256), pc * step:(pc + 1) * step]
                hi, lo = split(m)
                y = y_split[:, pc * step:(pc + 1) * step]
                p = lax.dot_general(y, hi, dims, preferred_element_type=jnp.float32)
                q = lax.dot_general(y[:rhs], lo, dims, preferred_element_type=jnp.float32)
                acc = acc + (p[:rhs] + (p[rhs:] + q))
            target[pl.ds(rt * 2 * TB, TB)] = acc[:, :LANES].reshape(TB, SUB, LANES)
            target[pl.ds(rt * 2 * TB + TB, TB)] = acc[:, LANES:].reshape(TB, SUB, LANES)
            return carry

        if chunk is not None:
            body(chunk, 0)
        else:
            lax.fori_loop(0, rows // 256, body, 0, unroll=2 if rows >= 512 else 1)

    for d in reversed(range(LEVELS)):
        group = leaf_group(d)
        G, me, _ = group
        loads["s", d].wait()
        if d < LEVELS - 1:
            prepare, sent = pend_scatter(d, group)

            def done(c, full):
                for half in range(2):
                    b = 2 * c + half
                    put_w(c, half, block_of(src[d], b) - block_of(full, b))

            _, finish = row_sum(f"w{d}", prepare, done)
            finish()
            sent()
        else:
            for b in range(nT // TB):
                put_w(b // 2, b % 2, block_of(src[d], b))
        loads["i", d].wait()
        if G > 1:
            over_rows(inv[d], nT // TB * LANES, cols[d], y_part)
            group_sum(f"y{d}", group, y_part, cols[d] // LANES * TB, y_full[d])
        else:
            over_rows(inv[d], nT // TB * LANES, cols[d], y_full[d])
        fill_y(lambda cb: block_of(y_full[d], cb), d)
        if d > 0:
            loads["u", d].wait()
            over_cols(upd[d], nb[d] * LANES, cols[d], c_buf)
            c_buf[pl.ds(nb[d] * TB, TB)] = jnp.zeros((TB, SUB, LANES), jnp.float32)
            first = cfg["inv_at"][d]

            def scatter(b, carry):
                j = index_ref[first + b]
                term = c_buf[pl.ds(j * TB, TB)]
                where = pl.ds(b * TB, TB)
                if d < LEVELS - 1:
                    term = pend[where] + term
                pend[where] = term
                return carry

            lax.fori_loop(0, base[d] // TB, scatter, 0, unroll=2)

    finals = []
    for d in range(LEVELS):
        group = leaf_group(d)
        G, me, _ = group
        if d > 0:
            first = cfg["idx_at"][d]

            def gather(pair, carry):
                for half in range(2):
                    b = index_ref[first + pair * 2 + half]
                    put_w(pair, half, stack[pl.ds(b * TB, TB)].reshape(rhs, LANES))
                return carry

            lax.fori_loop(0, nb[d] // 2, gather, 0, unroll=2)
            if G > 1:
                over_rows(upd[d], nb[d] * LANES, cols[d], y_part)
                group_sum(f"s{d}", group, y_part, cols[d] // LANES * TB, s_full[d])
            else:
                over_rows(upd[d], nb[d] * LANES, cols[d], s_full[d])
            fill_y(lambda cb: block_of(y_full[d], cb) - block_of(s_full[d], cb), d)
        if d < LEVELS - 1:
            done, gathered = front_gather(d, group)
        else:
            done = lambda c, full: None
        full, finish = row_sum(
            f"a{d}", lambda c: over_cols(inv[d], nT // TB * LANES, cols[d], z_part, c), done
        )
        final = pltpu.make_async_copy(full, out_hbm[d], out_sem.at[d])
        final.start()
        finals.append(final)
        if d < LEVELS - 1:
            gathered()
        finish()
    for final in finals:
        final.wait()


def hand_over(*refs):
    for d in range(LEVELS):
        refs[LEVELS + d][...] = refs[d][...]


def make_body(L, R):
    def body(*args):
        sources, inverse, update, links = args[0:4], args[4:8], (None,) + args[8:11], (None,) + args[11:14]
        own, rhs, lanes = sources[0].shape
        TB = rhs // SUB
        nT = own * TB
        blocks = own * L
        counts = [blocks >> d for d in range(LEVELS)]
        bases = [sum(counts[:d]) for d in range(LEVELS)]
        cols = [a.shape[2] for a in inverse]
        nb = [0] + [a.shape[0] for a in update[1:]]

        pieces = []
        idx_at, inv_at = [0] * LEVELS, [0] * LEVELS
        at = 0
        for d in range(1, LEVELS):
            link = links[d].astype(jnp.int32)
            level = link // blocks
            idx = jnp.zeros_like(link)
            for u in range(d):
                idx = jnp.where(level == u, bases[u] + link % counts[u], idx)
            idx_at[d] = at
            at += nb[d]
            number = jnp.arange(nb[d], dtype=jnp.int32)
            hits = idx[:, None] == jnp.arange(bases[d], dtype=jnp.int32)[None, :]
            inverse_map = nb[d] + jnp.sum(jnp.where(hits, (number - nb[d])[:, None], 0), axis=0)
            inv_at[d] = at
            at += bases[d]
            pieces += [idx, inverse_map.astype(jnp.int32)]
        index = jnp.concatenate(pieces)

        tile = lambda n: (n, SUB, LANES)
        phases = []
        C = max(1, own // 2)
        n_sems = 0
        for d in range(LEVELS):
            G = L >> d
            yt = cols[d] // LANES * TB
            kinds = ["a"]
            if d < LEVELS - 1:
                kinds.append("w")
                phases.append((f"pc{d}", G // 2 * nT))
                phases.append((f"ph{d}", max(1, (G // 2 - 1) * nT)))
                phases.append((f"fg{d}", G * nT))
                n_sems += 2 + G // 2 + C + 2 + C
            for kind in kinds:
                phases += [(kind + str(d) + part, nT) for part in "ixf"]
                n_sems += 2 + 3 * C
            if G > 1:
                n = yt if G == 2 else (G - 1) * (yt // G)
                phases.append((f"y{d}", n))
                n_sems += 4
                if d > 0:
                    phases.append((f"s{d}", n))
                    n_sems += 4
        cfg = dict(
            L=L, R=R, nT=nT, rhs=rhs, cols=cols, nb=nb, base=[b * TB for b in bases],
            idx_at=idx_at, inv_at=inv_at, phases=phases, C=C,
        )
        f32 = jnp.float32
        max_cols = max(cols)
        max_rows = max(max(nb), own)
        scratch = []
        scratch += [pltpu.VMEM(tile(nT), f32) for _ in range(LEVELS)]
        scratch += [pltpu.VMEM((a.shape[0] * a.shape[1], a.shape[2]), f32) for a in inverse]
        scratch += [pltpu.VMEM((a.shape[0] * a.shape[1], a.shape[2]), f32) for a in update[1:]]
        scratch.append(pltpu.VMEM(tile((max(nb) + 1) * TB), f32))
        scratch.append(pltpu.VMEM(tile(bases[-1] * TB), f32))
        scratch.append(pltpu.VMEM(tile(bases[-1] * TB), f32))
        scratch.append(pltpu.VMEM((max_rows // 2, 2 * rhs, 2 * LANES), jnp.bfloat16))
        scratch.append(pltpu.VMEM((2 * rhs, max_cols), jnp.bfloat16))
        scratch.append(pltpu.VMEM(tile(max_cols // LANES * TB), f32))
        scratch += [pltpu.VMEM(tile(cols[d] // LANES * TB), f32) for d in range(LEVELS)]
        scratch.append(pltpu.VMEM(tile(nT), f32))
        scratch += [pltpu.VMEM(tile(cols[d] // LANES * TB), f32) for d in range(1, LEVELS)]
        scratch.append(pltpu.SemaphoreType.DMA((3 * LEVELS,)))
        scratch.append(pltpu.SemaphoreType.DMA((LEVELS,)))
        scratch += [pltpu.VMEM(tile(n), f32) for _, n in phases]
        scratch.append(pltpu.SemaphoreType.DMA((n_sems,)))

        operands = [index]
        operands += [a.reshape(tile(nT)) for a in sources]
        operands += [a.reshape(-1, a.shape[2]) for a in inverse]
        operands += [a.reshape(-1, a.shape[2]) for a in update[1:]]
        anywhere = pl.BlockSpec(memory_space=pl.ANY)
        outs = pl.pallas_call(
            functools.partial(kernel, cfg),
            name="solve",
            out_shape=[jax.ShapeDtypeStruct(tile(nT), f32)] * LEVELS,
            in_specs=[pl.BlockSpec(memory_space=pltpu.SMEM)] + [anywhere] * (len(operands) - 1),
            out_specs=[anywhere] * LEVELS,
            scratch_shapes=scratch,
            compiler_params=pltpu.CompilerParams(
                collective_id=0, has_side_effects=True, vmem_limit_bytes=67043328 - (1 << 20)
            ),
        )(*operands)
        outs = pl.pallas_call(
            hand_over,
            name="hand_over",
            out_shape=[jax.ShapeDtypeStruct(tile(nT), f32)] * LEVELS,
            in_specs=[pl.BlockSpec(memory_space=pltpu.VMEM)] * LEVELS,
            out_specs=[pl.BlockSpec(memory_space=pltpu.VMEM)] * LEVELS,
        )(*outs)
        return tuple(o.reshape(own, rhs, lanes) for o in outs)

    return body


def solution(mesh):
    rows = P("leaf", None, None)
    factor = P("leaf", None, "row")
    return jax.shard_map(
        make_body(mesh.shape["leaf"], mesh.shape["row"]),
        mesh=mesh,
        in_specs=(rows,) * 4 + (factor,) * 7 + (P("leaf"),) * 3,
        out_specs=(rows,) * 4,
        check_vma=False,
    )
```

```python
import functools

import jax
import jax.numpy as jnp
from jax import lax
from jax.experimental import pallas as pl
from jax.experimental.pallas import tpu as pltpu
from jax.sharding import PartitionSpec as P

LANES = 128
SUB = 8
MESH = pl.DeviceIdType.MESH
LEVELS = 4


def split(x):
    hi = x.astype(jnp.bfloat16)
    lo = (x - hi.astype(jnp.float32)).astype(jnp.bfloat16)
    return hi, lo


def kernel(cfg, *refs):
    L, R = cfg["L"], cfg["R"]
    nT = cfg["nT"]
    rhs = cfg["rhs"]
    TB = rhs // SUB
    cols = cfg["cols"]
    nb = cfg["nb"]
    base = cfg["base"]
    it = iter(refs)
    index_ref = next(it)
    src_hbm = [next(it) for _ in range(LEVELS)]
    inv_hbm = [next(it) for _ in range(LEVELS)]
    upd_hbm = [None] + [next(it) for _ in range(LEVELS - 1)]
    out_hbm = [next(it) for _ in range(LEVELS)]
    src = [next(it) for _ in range(LEVELS)]
    inv = [next(it) for _ in range(LEVELS)]
    upd = [None] + [next(it) for _ in range(LEVELS - 1)]
    c_buf = next(it)
    pend = next(it)
    stack = next(it)
    w_split = next(it)
    y_split = next(it)
    y_part = next(it)
    y_full = [next(it) for _ in range(LEVELS)]
    z_part = next(it)
    s_full = [None] + [next(it) for _ in range(LEVELS - 1)]
    load_sem = next(it)
    out_sem = next(it)
    phases = {}
    for name, _ in cfg["phases"]:
        phases[name] = next(it)
    sems = next(it)

    leaf = lax.axis_index("leaf")
    row = lax.axis_index("row")

    loads = {}
    at = 0
    for d in reversed(range(LEVELS)):
        for tag, a, b in (("s", src_hbm, src), ("i", inv_hbm, inv), ("u", upd_hbm, upd)):
            if a[d] is None:
                continue
            copy = pltpu.make_async_copy(a[d], b[d], load_sem.at[at])
            copy.start()
            loads[tag, d] = copy
            at += 1

    barrier = pltpu.get_barrier_semaphore()
    for k in range(1, L):
        pl.semaphore_signal(barrier, inc=1, device_id=((leaf + k) % L, row), device_id_type=MESH)
    for k in range(1, R):
        pl.semaphore_signal(barrier, inc=1, device_id=(leaf, (row + k) % R), device_id_type=MESH)
    pl.semaphore_wait(barrier, L + R - 2)

    def leaf_group(d):
        G = L >> d
        first = (leaf // G) * G
        me = leaf % G
        return G, me, lambda other: (first + other, row)

    def tiles(ref, start, n):
        return ref.at[pl.ds(start, n)]

    counter = [0]

    def new_sem():
        counter[0] += 1
        return sems.at[counter[0] - 1]

    def wait_tiles(sem, ref, n):
        whole = ref.at[pl.ds(0, n)]
        pltpu.make_async_copy(whole, whole, sem).wait()

    def push(source, target, out_s, in_s, device):
        pltpu.make_async_remote_copy(
            src_ref=source,
            dst_ref=target,
            send_sem=out_s,
            recv_sem=in_s,
            device_id=device,
            device_id_type=MESH,
        ).start()

    def group_sum(name, group, source, total_tiles, target, compute):
        G, me, who = group
        recv = phases[name]
        if G == 2:
            compute(None)
            out_s, in_s = new_sem(), new_sem()
            push(tiles(source, 0, total_tiles), tiles(recv, 0, total_tiles), out_s, in_s, who(1 - me))
            wait_tiles(in_s, recv, total_tiles)
            target[...] = source[pl.ds(0, total_tiles)] + recv[...]
            wait_tiles(out_s, recv, total_tiles)
            return
        n = total_tiles // G
        out_s, in_s = new_sem(), new_sem()

        def ready(start, stop):
            for other in range(start // n, stop // n):
                @pl.when(me != other)
                def _():
                    slot = (other - me + G) % G - 1
                    push(tiles(source, other * n, n), tiles(recv, slot * n, n), out_s, in_s, who(other))

        compute(ready)
        wait_tiles(in_s, recv, (G - 1) * n)
        total = source[pl.ds(me * n, n)]
        for k in range(1, G):
            total = total + recv[pl.ds((k - 1) * n, n)]
        target[pl.ds(me * n, n)] = total
        wait_tiles(out_s, recv, (G - 1) * n)
        out_s, in_s = new_sem(), new_sem()
        for k in range(1, G):
            mine = tiles(target, me * n, n)
            push(mine, mine, out_s, in_s, who((me + k) % G))
        wait_tiles(in_s, target, (G - 1) * n)
        wait_tiles(out_s, target, (G - 1) * n)

    C, cn = cfg["C"], nT // cfg["C"]
    half_row = R // 2
    right = row // half_row
    inward = row + 1 - 2 * right
    outward = row - 1 + 2 * right
    depth = (half_row - 1 - row) * (1 - right) + (row - half_row) * right

    def row_sum(name, prepare, done):
        came, across, full = phases[name + "i"], phases[name + "x"], phases[name + "f"]
        out_in, out_back = new_sem(), new_sem()
        in_s = [new_sem() for _ in range(C)]
        x_s = [new_sem() for _ in range(C)]
        f_s = [new_sem() for _ in range(C)]
        for c in range(C):
            part = tiles(z_part, c * cn, cn)
            prepare(c)
            if half_row > 1:
                @pl.when(depth < half_row - 1)
                def _():
                    wait_tiles(in_s[c], came, cn)
                    z_part[pl.ds(c * cn, cn)] = z_part[pl.ds(c * cn, cn)] + came[pl.ds(c * cn, cn)]

                @pl.when(depth > 0)
                def _():
                    push(part, tiles(came, c * cn, cn), out_in, in_s[c], (leaf, inward))

            @pl.when(depth == 0)
            def _():
                push(part, tiles(across, c * cn, cn), out_in, x_s[c], (leaf, inward))
        for c in range(C):
            here = tiles(full, c * cn, cn)

            @pl.when(depth == 0)
            def _():
                wait_tiles(x_s[c], across, cn)
                full[pl.ds(c * cn, cn)] = z_part[pl.ds(c * cn, cn)] + across[pl.ds(c * cn, cn)]

            if half_row > 1:
                @pl.when(depth > 0)
                def _():
                    wait_tiles(f_s[c], full, cn)

                @pl.when(depth < half_row - 1)
                def _():
                    push(here, here, out_back, f_s[c], (leaf, outward))
            done(c, full)

        def finish():
            wait_tiles(out_in, full, nT)
            if half_row > 1:
                @pl.when(depth < half_row - 1)
                def _():
                    wait_tiles(out_back, full, nT)

        return full, finish

    def pend_scatter(d, group):
        G, me, who = group
        H, chip, core = G // 2, me // 2, me % 2
        from_core, from_chip = phases[f"pc{d}"], phases[f"ph{d}"]
        out_core, out_chip = new_sem(), new_sem()
        core_s = [new_sem() for _ in range(H)]
        chip_s = [new_sem() for _ in range(C)]
        for k in list(range(1, H)) + [0]:
            ch = (chip + k) % H
            push(tiles(pend, base[d] + (2 * ch + 1 - core) * nT, nT), tiles(from_core, k * nT, nT), out_core, core_s[k], who(2 * chip + 1 - core))
        for c in range(C):
            for k in range(1, H):
                ch = (chip + k) % H
                if c == 0:
                    wait_tiles(core_s[k], from_core, nT)
                where = pl.ds(base[d] + (2 * ch + core) * nT + c * cn, cn)
                pend[where] = pend[where] + from_core[pl.ds(k * nT + c * cn, cn)]
                push(pend.at[where], tiles(from_chip, (k - 1) * nT + c * cn, cn), out_chip, chip_s[c], who(2 * ch + core))

        def prepare(c):
            if c == 0:
                wait_tiles(core_s[0], from_core, nT)
            total = pend[pl.ds(base[d] + me * nT + c * cn, cn)] + from_core[pl.ds(c * cn, cn)]
            if H > 1:
                wait_tiles(chip_s[c], from_chip, (H - 1) * cn)
            for k in range(1, H):
                total = total + from_chip[pl.ds((k - 1) * nT + c * cn, cn)]
            z_part[pl.ds(c * cn, cn)] = total

        def finish():
            wait_tiles(out_core, pend, H * nT)
            if H > 1:
                wait_tiles(out_chip, pend, (H - 1) * nT)

        return prepare, finish

    def front_gather(d, group):
        G, me, who = group
        H, chip, core = G // 2, me // 2, me % 2
        front = phases[f"fg{d}"]
        out_s, core_s = new_sem(), new_sem()
        chip_s = [new_sem() for _ in range(C)]
        partner = who(2 * chip + 1 - core)

        def done(c, full):
            mine = tiles(full, c * cn, cn)
            target = tiles(front, me * nT + c * cn, cn)
            for k in range(1, H):
                push(mine, target, out_s, chip_s[c], who(2 * ((chip + k) % H) + core))
            push(mine, target, out_s, core_s, partner)
            front[pl.ds(me * nT + c * cn, cn)] = full[pl.ds(c * cn, cn)]

        def finish():
            for c in range(C):
                if H > 1:
                    wait_tiles(chip_s[c], front, (H - 1) * cn)
                for k in range(1, H):
                    other = 2 * ((chip + k) % H) + core
                    piece = tiles(front, other * nT + c * cn, cn)
                    push(piece, piece, out_s, core_s, partner)
            wait_tiles(core_s, front, H * nT)
            wait_tiles(out_s, front, (2 * H - 1) * nT)
            stack[pl.ds(base[d], G * nT)] = front[...]

        return done, finish

    def put_w(pair, half, block):
        hi, lo = split(block)
        w_split[pair, 0:rhs, half * LANES:(half + 1) * LANES] = hi
        w_split[pair, rhs:2 * rhs, half * LANES:(half + 1) * LANES] = lo

    def fill_y(values, d):
        for cb in range(cols[d] // LANES):
            hi, lo = split(values(cb))
            y_split[0:rhs, cb * LANES:(cb + 1) * LANES] = hi
            y_split[rhs:2 * rhs, cb * LANES:(cb + 1) * LANES] = lo

    def block_of(ref, b):
        return ref[pl.ds(b * TB, TB)].reshape(rhs, LANES)

    def over_rows(mat, rows, width, target, ready=None):
        step = min(512, width)
        for nt in range(width // step):
            def body(k, acc):
                m = mat[pl.ds(k * 256, 256), nt * step:(nt + 1) * step]
                hi, lo = split(m)
                w = w_split[k]
                p = jnp.dot(w, hi, preferred_element_type=jnp.float32)
                q = jnp.dot(w[:rhs], lo, preferred_element_type=jnp.float32)
                return acc + (p[:rhs] + (p[rhs:] + q))
            acc = lax.fori_loop(0, rows // 256, body, jnp.zeros((rhs, step), jnp.float32), unroll=2 if rows >= 512 else 1)
            for c in range(step // LANES):
                target[pl.ds((nt * (step // LANES) + c) * TB, TB)] = acc[:, c * LANES:(c + 1) * LANES].reshape(TB, SUB, LANES)
            if ready is not None:
                per = step // LANES * TB
                ready(nt * per, (nt + 1) * per)

    def over_cols(mat, rows, width, target, chunk=None):
        step = min(512, width)
        dims = (((1,), (1,)), ((), ()))

        def body(rt, carry):
            acc = jnp.zeros((rhs, 256), jnp.float32)
            for pc in range(width // step):
                m = mat[pl.ds(rt * 256, 256), pc * step:(pc + 1) * step]
                hi, lo = split(m)
                y = y_split[:, pc * step:(pc + 1) * step]
                p = lax.dot_general(y, hi, dims, preferred_element_type=jnp.float32)
                q = lax.dot_general(y[:rhs], lo, dims, preferred_element_type=jnp.float32)
                acc = acc + (p[:rhs] + (p[rhs:] + q))
            target[pl.ds(rt * 2 * TB, TB)] = acc[:, :LANES].reshape(TB, SUB, LANES)
            target[pl.ds(rt * 2 * TB + TB, TB)] = acc[:, LANES:].reshape(TB, SUB, LANES)
            return carry

        if chunk is not None:
            body(chunk, 0)
        else:
            lax.fori_loop(0, rows // 256, body, 0, unroll=2 if rows >= 512 else 1)

    for d in reversed(range(LEVELS)):
        group = leaf_group(d)
        G, me, _ = group
        loads["s", d].wait()
        if d < LEVELS - 1:
            prepare, sent = pend_scatter(d, group)

            def done(c, full):
                for half in range(2):
                    b = 2 * c + half
                    put_w(c, half, block_of(src[d], b) - block_of(full, b))

            _, finish = row_sum(f"w{d}", prepare, done)
            finish()
            sent()
        else:
            for b in range(nT // TB):
                put_w(b // 2, b % 2, block_of(src[d], b))
        loads["i", d].wait()
        if G > 1:
            group_sum(
                f"y{d}", group, y_part, cols[d] // LANES * TB, y_full[d],
                lambda ready: over_rows(inv[d], nT // TB * LANES, cols[d], y_part, ready),
            )
        else:
            over_rows(inv[d], nT // TB * LANES, cols[d], y_full[d])
        fill_y(lambda cb: block_of(y_full[d], cb), d)
        if d > 0:
            loads["u", d].wait()
            over_cols(upd[d], nb[d] * LANES, cols[d], c_buf)
            c_buf[pl.ds(nb[d] * TB, TB)] = jnp.zeros((TB, SUB, LANES), jnp.float32)
            first = cfg["inv_at"][d]

            def scatter(b, carry):
                j = index_ref[first + b]
                term = c_buf[pl.ds(j * TB, TB)]
                where = pl.ds(b * TB, TB)
                if d < LEVELS - 1:
                    term = pend[where] + term
                pend[where] = term
                return carry

            lax.fori_loop(0, base[d] // TB, scatter, 0, unroll=2)

    finals = []
    for d in range(LEVELS):
        group = leaf_group(d)
        G, me, _ = group
        if d > 0:
            first = cfg["idx_at"][d]

            def gather(pair, carry):
                for half in range(2):
                    b = index_ref[first + pair * 2 + half]
                    put_w(pair, half, stack[pl.ds(b * TB, TB)].reshape(rhs, LANES))
                return carry

            lax.fori_loop(0, nb[d] // 2, gather, 0, unroll=2)
            if G > 1:
                group_sum(
                    f"s{d}", group, y_part, cols[d] // LANES * TB, s_full[d],
                    lambda ready: over_rows(upd[d], nb[d] * LANES, cols[d], y_part, ready),
                )
            else:
                over_rows(upd[d], nb[d] * LANES, cols[d], s_full[d])
            fill_y(lambda cb: block_of(y_full[d], cb) - block_of(s_full[d], cb), d)
        if d < LEVELS - 1:
            done, gathered = front_gather(d, group)
        else:
            done = lambda c, full: None
        full, finish = row_sum(
            f"a{d}", lambda c: over_cols(inv[d], nT // TB * LANES, cols[d], z_part, c), done
        )
        final = pltpu.make_async_copy(full, out_hbm[d], out_sem.at[d])
        final.start()
        finals.append(final)
        if d < LEVELS - 1:
            gathered()
        finish()
    for final in finals:
        final.wait()


def hand_over(*refs):
    for d in range(LEVELS):
        refs[LEVELS + d][...] = refs[d][...]


def make_body(L, R):
    def body(*args):
        sources, inverse, update, links = args[0:4], args[4:8], (None,) + args[8:11], (None,) + args[11:14]
        own, rhs, lanes = sources[0].shape
        TB = rhs // SUB
        nT = own * TB
        blocks = own * L
        counts = [blocks >> d for d in range(LEVELS)]
        bases = [sum(counts[:d]) for d in range(LEVELS)]
        cols = [a.shape[2] for a in inverse]
        nb = [0] + [a.shape[0] for a in update[1:]]

        pieces = []
        idx_at, inv_at = [0] * LEVELS, [0] * LEVELS
        at = 0
        for d in range(1, LEVELS):
            link = links[d].astype(jnp.int32)
            level = link // blocks
            idx = jnp.zeros_like(link)
            for u in range(d):
                idx = jnp.where(level == u, bases[u] + link % counts[u], idx)
            idx_at[d] = at
            at += nb[d]
            number = jnp.arange(nb[d], dtype=jnp.int32)
            hits = idx[:, None] == jnp.arange(bases[d], dtype=jnp.int32)[None, :]
            inverse_map = nb[d] + jnp.sum(jnp.where(hits, (number - nb[d])[:, None], 0), axis=0)
            inv_at[d] = at
            at += bases[d]
            pieces += [idx, inverse_map.astype(jnp.int32)]
        index = jnp.concatenate(pieces)

        tile = lambda n: (n, SUB, LANES)
        phases = []
        C = max(1, own // 2)
        n_sems = 0
        for d in range(LEVELS):
            G = L >> d
            yt = cols[d] // LANES * TB
            kinds = ["a"]
            if d < LEVELS - 1:
                kinds.append("w")
                phases.append((f"pc{d}", G // 2 * nT))
                phases.append((f"ph{d}", max(1, (G // 2 - 1) * nT)))
                phases.append((f"fg{d}", G * nT))
                n_sems += 2 + G // 2 + C + 2 + C
            for kind in kinds:
                phases += [(kind + str(d) + part, nT) for part in "ixf"]
                n_sems += 2 + 3 * C
            if G > 1:
                n = yt if G == 2 else (G - 1) * (yt // G)
                phases.append((f"y{d}", n))
                n_sems += 4
                if d > 0:
                    phases.append((f"s{d}", n))
                    n_sems += 4
        cfg = dict(
            L=L, R=R, nT=nT, rhs=rhs, cols=cols, nb=nb, base=[b * TB for b in bases],
            idx_at=idx_at, inv_at=inv_at, phases=phases, C=C,
        )
        f32 = jnp.float32
        max_cols = max(cols)
        max_rows = max(max(nb), own)
        scratch = []
        scratch += [pltpu.VMEM(tile(nT), f32) for _ in range(LEVELS)]
        scratch += [pltpu.VMEM((a.shape[0] * a.shape[1], a.shape[2]), f32) for a in inverse]
        scratch += [pltpu.VMEM((a.shape[0] * a.shape[1], a.shape[2]), f32) for a in update[1:]]
        scratch.append(pltpu.VMEM(tile((max(nb) + 1) * TB), f32))
        scratch.append(pltpu.VMEM(tile(bases[-1] * TB), f32))
        scratch.append(pltpu.VMEM(tile(bases[-1] * TB), f32))
        scratch.append(pltpu.VMEM((max_rows // 2, 2 * rhs, 2 * LANES), jnp.bfloat16))
        scratch.append(pltpu.VMEM((2 * rhs, max_cols), jnp.bfloat16))
        scratch.append(pltpu.VMEM(tile(max_cols // LANES * TB), f32))
        scratch += [pltpu.VMEM(tile(cols[d] // LANES * TB), f32) for d in range(LEVELS)]
        scratch.append(pltpu.VMEM(tile(nT), f32))
        scratch += [pltpu.VMEM(tile(cols[d] // LANES * TB), f32) for d in range(1, LEVELS)]
        scratch.append(pltpu.SemaphoreType.DMA((3 * LEVELS,)))
        scratch.append(pltpu.SemaphoreType.DMA((LEVELS,)))
        scratch += [pltpu.VMEM(tile(n), f32) for _, n in phases]
        scratch.append(pltpu.SemaphoreType.DMA((n_sems,)))

        operands = [index]
        operands += [a.reshape(tile(nT)) for a in sources]
        operands += [a.reshape(-1, a.shape[2]) for a in inverse]
        operands += [a.reshape(-1, a.shape[2]) for a in update[1:]]
        anywhere = pl.BlockSpec(memory_space=pl.ANY)
        outs = pl.pallas_call(
            functools.partial(kernel, cfg),
            name="solve",
            out_shape=[jax.ShapeDtypeStruct(tile(nT), f32)] * LEVELS,
            in_specs=[pl.BlockSpec(memory_space=pltpu.SMEM)] + [anywhere] * (len(operands) - 1),
            out_specs=[anywhere] * LEVELS,
            scratch_shapes=scratch,
            compiler_params=pltpu.CompilerParams(
                collective_id=0, has_side_effects=True, vmem_limit_bytes=67043328 - (1 << 20)
            ),
        )(*operands)
        outs = pl.pallas_call(
            hand_over,
            name="hand_over",
            out_shape=[jax.ShapeDtypeStruct(tile(nT), f32)] * LEVELS,
            in_specs=[pl.BlockSpec(memory_space=pltpu.VMEM)] * LEVELS,
            out_specs=[pl.BlockSpec(memory_space=pltpu.VMEM)] * LEVELS,
        )(*outs)
        return tuple(o.reshape(own, rhs, lanes) for o in outs)

    return body


def solution(mesh):
    rows = P("leaf", None, None)
    factor = P("leaf", None, "row")
    return jax.shard_map(
        make_body(mesh.shape["leaf"], mesh.shape["row"]),
        mesh=mesh,
        in_specs=(rows,) * 4 + (factor,) * 7 + (P("leaf"),) * 3,
        out_specs=(rows,) * 4,
        check_vma=False,
    )
```
